256 devices in a mesh: frame: 32 (over y, z), head: 8 (over x, core).
Axes of the slice: x: 4, y: 4, z: 8, core: 2. Of those that a mesh axis runs over, the one named last changes fastest.
Arguments:
- queries: bfloat16 [4096, 1024], P(None, 'head'), may hold values from -8 to 8
- keys: bfloat16 [65536, 1024], P(('frame', 'head')), may hold values from -8 to 8
- values: bfloat16 [65536, 1024], P(('frame', 'head')), may hold values from -6 to 6
Outputs:
- attended: bfloat16 [4096, 1024], P('frame', 'head')
The draws below stay inside these ranges and needn't reach their ends.
All inputs are finite; a program needn't handle non-finite values.
Results may differ from the reference program's by a relative error of at most 0.0049.
Values may be sent and summed in bfloat16 or wider, within the bound.
No kernel may reach another device: no remote copies, remote signals or barrier semaphores. Data moves between devices by JAX's collectives and lax.ppermute only.
A program may use at most 64 MiB of HBM per device.

```python
import jax
import jax.numpy as jnp
from jax import lax

HEADS = 16
HEAD_DIM = 64
D = 1024
NQ = 4096
NF = 65536


def draw_keys(key, part):
    own = jax.random.fold_in(key, 101)
    base = jnp.clip(jax.random.normal(own, (NF, D), jnp.float32), -4.0, 4.0)
    return base.astype(jnp.bfloat16)


def draw_queries(key, part):
    own = jax.random.fold_in(key, 202)
    base = jnp.clip(jax.random.normal(own, (NQ, D), jnp.float32), -4.0, 4.0)
    return base.astype(jnp.bfloat16)


def level_of(rng, dims, split, least, largest):
    def one(position, parts):
        draws = jax.random.uniform(jax.random.fold_in(jax.random.fold_in(rng, 6), position), (parts,), jnp.float32, least / len(split), largest / len(split))
        return jnp.repeat(jnp.exp(draws), dims[position] // parts).reshape((-1,) + (1,) * (len(dims) - position - 1))

    gain = one(*split[0])
    for cut in split[1:]:
        gain = gain * one(*cut)
    return gain


def scatter_about(own_key, extent, scale, reach, pieces=(), held_as=jnp.bfloat16):
    values = jax.random.normal(own_key, extent, jnp.float32) * scale
    if len(pieces) > 0:
        values = level_of(own_key, extent, pieces, -0.22, 0.18) * values
    return jnp.clip(values, min=-reach, max=reach).astype(held_as)


def setup_inputs(seed: int = 0) -> dict:
    streams_of = jax.random.split(jax.random.key(seed), 4)
    queries = draw_queries(jax.random.fold_in(streams_of[3], 71), 0)
    keys = draw_keys(jax.random.fold_in(streams_of[3], 71), 0)
    values = scatter_about(streams_of[2], (NF, D), 1.0, 6.0, ((0, 256),))
    return dict(queries=queries, keys=keys, values=values)


def reference(queries, keys, values):
    scale = HEAD_DIM ** -0.5
    qblock = min(256, NQ)
    turns = NQ // qblock

    def one_head(head):
        start = (head * HEAD_DIM).astype(jnp.int32)
        q_head = lax.dynamic_slice_in_dim(queries, start, HEAD_DIM, 1)
        k_head = lax.dynamic_slice_in_dim(keys, start, HEAD_DIM, 1)
        v_head = lax.dynamic_slice_in_dim(values, start, HEAD_DIM, 1)
        k_trans = k_head.T
        q_blocks = q_head.reshape(turns, qblock, HEAD_DIM)

        def one_block(q_rows):
            scores = jnp.dot(q_rows, k_trans, preferred_element_type=jnp.float32) * scale
            top = jnp.max(scores, axis=1, keepdims=True)
            weights = jnp.exp(scores - top)
            total = jnp.sum(weights, axis=1, keepdims=True)
            mixed = jnp.dot(weights.astype(jnp.bfloat16), v_head, preferred_element_type=jnp.float32)
            return mixed / total

        return lax.map(one_block, q_blocks).reshape(NQ, HEAD_DIM)

    heads_out = lax.map(one_head, jnp.arange(HEADS, dtype=jnp.int32))
    return jnp.transpose(heads_out, (1, 0, 2)).reshape(NQ, D).astype(jnp.bfloat16)
```

```python
import functools

import jax
import jax.numpy as jnp
from jax import lax
from jax.experimental import pallas as pl
from jax.experimental.pallas import tpu as pltpu
from jax.sharding import PartitionSpec as P

HEAD_DIM = 64
HEADS_HERE = 2
RIM = 16
ROWS = HEAD_DIM + RIM
SCALE = 1.4426950408889634 * HEAD_DIM ** (-0.5)
Y = 4
Z = 8
TILE = 512
BF = jnp.bfloat16
F32 = jnp.float32
VMEM = pl.BlockSpec(memory_space=pltpu.VMEM)


def call(body, inputs, outs, name, scratch=(), flops=0, exps=0):
    return pl.pallas_call(
        body,
        out_shape=outs,
        in_specs=[VMEM] * len(inputs),
        out_specs=jax.tree.map(lambda _: VMEM, outs),
        scratch_shapes=list(scratch),
        name=name,
        compiler_params=pltpu.CompilerParams(vmem_limit_bytes=40 << 20),
        cost_estimate=pl.CostEstimate(flops=flops, transcendentals=exps, bytes_accessed=1 << 20),
    )(*inputs)


def pack_body(keys, values, first, second):
    for j in range(first.shape[0]):
        k = keys[:, 128 * j : 128 * j + 128]
        v = values[:, 128 * j : 128 * j + 128]
        first[j] = jnp.concatenate([k[:, :HEAD_DIM], v[:, :HEAD_DIM]], axis=1)
        second[j] = jnp.concatenate([k[:, HEAD_DIM:], v[:, HEAD_DIM:]], axis=1)


def turn_body(queries, first, second):
    count = queries.shape[0]
    for i in range(0, count, TILE):
        t = queries[i : i + TILE, :].T
        none = jnp.zeros((HEAD_DIM, TILE), BF)
        first[:HEAD_DIM, i : i + TILE] = t[:HEAD_DIM]
        first[HEAD_DIM:, i : i + TILE] = none
        second[:HEAD_DIM, i : i + TILE] = t[HEAD_DIM:]
        second[HEAD_DIM:, i : i + TILE] = none


def prep_body(pairs, out):
    t = pairs[...].T
    out[:HEAD_DIM] = t[HEAD_DIM:]
    out[HEAD_DIM:] = jnp.ones((RIM, t.shape[1]), BF)


def write_rim(lse):
    high = lse.astype(BF).astype(F32)
    rest = lse - high
    mid = rest.astype(BF).astype(F32)
    low = rest - mid
    row = lax.broadcasted_iota(jnp.int32, (RIM, lse.shape[1]), 0)
    return jnp.where(row == 0, high, jnp.where(row == 1, mid, jnp.where(row == 2, low, 0.0)))


def attend_body(shifts, queries, pairs, turned, *rest):
    outs, (even, odd) = rest[: len(shifts)], rest[len(shifts) :]
    block = outs[0].shape[1]
    y = lax.axis_index("frame") // Z
    tiles = [(b, i) for b in range(len(shifts)) for i in range(block // TILE)]

    def score(t, held):
        b, i = tiles[t]
        start = pl.multiple_of(lax.rem(y + shifts[b], Y) * block + i * TILE, TILE)
        held[...] = jnp.dot(
            pairs[...], queries[:, pl.ds(start, TILE)], preferred_element_type=F32
        )

    def gather(t, held):
        b, i = tiles[t]
        top = jnp.max(held[...], axis=0, keepdims=True) * SCALE
        weights = jnp.exp2(held[...] * SCALE - top).astype(BF)
        mixed = jnp.dot(turned[...], weights, preferred_element_type=F32)
        total = mixed[HEAD_DIM : HEAD_DIM + 1]
        span = slice(i * TILE, i * TILE + TILE)
        outs[b][:HEAD_DIM, span] = (mixed[:HEAD_DIM] / total).astype(BF)
        outs[b][HEAD_DIM:, span] = write_rim(top + jnp.log2(total)).astype(BF)

    score(0, even)
    for t in range(len(tiles)):
        here, there = (even, odd) if t % 2 == 0 else (odd, even)
        if t + 1 < len(tiles):
            score(t + 1, there)
        gather(t, here)


def attend(shifts, queries, pairs, turned, block):
    rows = pairs.shape[0]
    outs = [jax.ShapeDtypeStruct((ROWS, block), BF) for _ in shifts]
    work = len(shifts) * block * rows
    return call(
        functools.partial(attend_body, shifts),
        (queries, pairs, turned),
        outs,
        "attend",
        scratch=[pltpu.VMEM((rows, TILE), F32)] * 2,
        flops=work * 512,
        exps=work,
    )


def merge(parts):
    logs = [jnp.sum(p[HEAD_DIM:].astype(F32), axis=0, keepdims=True) for p in parts]
    top = functools.reduce(jnp.maximum, logs)
    shares = [jnp.exp2(l - top) for l in logs]
    total = functools.reduce(jnp.add, shares)
    mixed = functools.reduce(
        jnp.add, [p[:HEAD_DIM].astype(F32) * s for p, s in zip(parts, shares)]
    )
    return mixed / total, top + jnp.log2(total)


def merge_body(cuts, position, parts, *refs):
    ins, outs = refs[:parts], refs[parts:]
    width = outs[0].shape[1]
    me = position()
    for k, out in enumerate(outs):
        start = pl.multiple_of(lax.rem(me + k, cuts) * width, width)
        mixed, lse = merge([r[:, pl.ds(start, width)] for r in ins])
        out[:HEAD_DIM] = mixed.astype(BF)
        out[HEAD_DIM:] = write_rim(lse).astype(BF)


def split_merge(parts, cuts, position):
    width = parts[0].shape[1] // cuts
    outs = [jax.ShapeDtypeStruct((ROWS, width), BF) for _ in range(cuts)]
    return call(
        functools.partial(merge_body, cuts, position, len(parts)), parts, outs, "merge"
    )


def last_body(first_a, first_b, second_a, second_b, out):
    first, unused = merge([first_a[...], first_b[...]])
    second, unused = merge([second_a[...], second_b[...]])
    out[...] = jnp.concatenate([first, second], axis=0).T.astype(BF)


def move(x, target):
    return lax.ppermute(x, "frame", [(f, target(f // Z, f % Z)) for f in range(Y * Z)])


def half_of_z():
    return lax.rem(lax.axis_index("frame"), Z) // 2


def odd_of_z():
    return lax.rem(lax.axis_index("frame"), 2)


def local(queries, keys, values):
    count = queries.shape[0]
    block = count // Y
    ranks = lax.axis_size("head")
    tokens = keys.shape[0]
    sent = call(
        pack_body,
        (keys, values),
        [jax.ShapeDtypeStruct((ranks, tokens, 128), BF)] * HEADS_HERE,
        "pack",
    )
    arrived = [lax.all_to_all(x, "head", 0, 0, tiled=True) for x in sent]
    turned_queries = call(
        turn_body, (queries,), [jax.ShapeDtypeStruct((128, count), BF)] * HEADS_HERE, "turn"
    )
    ends = []
    for head in range(HEADS_HERE):
        pairs = arrived[head].reshape(ranks * tokens, 128)
        turned = call(
            prep_body, (pairs,), jax.ShapeDtypeStruct((ROWS, ranks * tokens), BF), "prep"
        )
        parts = []
        for shift in (2, 1, 3, 0):
            (part,) = attend((shift,), turned_queries[head], pairs, turned, block)
            if shift:
                part = move(part, lambda y, z: (y + shift) % Y * Z + z)
            parts.append(part)
        pieces = split_merge(parts, Z // 2, half_of_z)
        parts = [pieces[0]]
        for k in range(1, Z // 2):
            parts.append(move(pieces[k], lambda y, z: y * Z + (z + 2 * k) % Z))
        mine, other = split_merge(parts, 2, odd_of_z)
        ends += [mine, move(other, lambda y, z: y * Z + (z ^ 1))]
    return call(last_body, ends, jax.ShapeDtypeStruct((count // Y // Z, 128), BF), "last")


def solution(mesh):
    placed = (P(None, "head"), P(("frame", "head"), None), P(("frame", "head"), None))
    return jax.shard_map(
        local, mesh=mesh, in_specs=placed, out_specs=P("frame", "head"), check_vma=False
    )
```

```python
import functools

import jax
import jax.numpy as jnp
from jax import lax
from jax.experimental import pallas as pl
from jax.experimental.pallas import tpu as pltpu
from jax.sharding import Mesh
from jax.sharding import PartitionSpec as P

HEAD_DIM = 64
RIM = 16
FLAT = 8
ROWS = HEAD_DIM + RIM
SCALE = 1.4426950408889634 * HEAD_DIM ** (-0.5)
Y, A, B = 4, 4, 2
TILE = 512
BF = jnp.bfloat16
F32 = jnp.float32
VMEM = pl.BlockSpec(memory_space=pltpu.VMEM)


def call(body, inputs, outs, name, scratch=(), room=16, flops=0):
    return pl.pallas_call(
        body,
        out_shape=outs,
        in_specs=[VMEM] * len(inputs),
        out_specs=jax.tree.map(lambda _: VMEM, outs),
        scratch_shapes=list(scratch),
        name=name,
        compiler_params=pltpu.CompilerParams(vmem_limit_bytes=room << 20),
        cost_estimate=pl.CostEstimate(flops=flops, transcendentals=0, bytes_accessed=1 << 18),
    )(*inputs)


def pack_body(keys, values, out):
    ranks = out.shape[0] // 2
    for j in range(ranks):
        k = keys[:, 128 * j : 128 * j + 128]
        v = values[:, 128 * j : 128 * j + 128]
        out[j] = jnp.concatenate([k[:, :HEAD_DIM], v[:, :HEAD_DIM]], axis=1)
        out[ranks + j] = jnp.concatenate([k[:, HEAD_DIM:], v[:, HEAD_DIM:]], axis=1)


def turn_body(queries, out):
    count = queries.shape[0]
    second = lax.axis_index("b") == 1
    out[HEAD_DIM:] = jnp.zeros((HEAD_DIM, count), BF)
    for i in range(0, count, TILE):
        t = queries[i : i + TILE, :].T
        out[:HEAD_DIM, i : i + TILE] = jnp.where(second, t[HEAD_DIM:], t[:HEAD_DIM])


def prep_body(pairs, out):
    t = pairs[...].T
    out[:HEAD_DIM] = t[HEAD_DIM:]
    out[HEAD_DIM:] = jnp.ones((RIM, t.shape[1]), BF)


def write_rim(lse):
    high = lse.astype(BF).astype(F32)
    rest = lse - high
    mid = rest.astype(BF).astype(F32)
    low = rest - mid
    row = lax.broadcasted_iota(jnp.int32, (RIM, lse.shape[1]), 0)
    return jnp.where(row == 0, high, jnp.where(row == 1, mid, jnp.where(row == 2, low, 0.0)))


def attend_body(shifts, queries, pairs, turned, *rest):
    outs, (even, odd) = rest[: len(shifts)], rest[len(shifts) :]
    block = outs[0].shape[1]
    y = lax.axis_index("y")
    tiles = [(b, i) for b in range(len(shifts)) for i in range(block // TILE)]

    def score(t, held):
        b, i = tiles[t]
        start = pl.multiple_of(lax.rem(y + shifts[b], Y) * block + i * TILE, TILE)
        held[...] = jnp.dot(
            pairs[...], queries[:, pl.ds(start, TILE)], preferred_element_type=F32
        )

    def gather(t, held):
        b, i = tiles[t]
        top = jnp.max(held[...], axis=0, keepdims=True) * SCALE
        weights = jnp.exp2(held[...] * SCALE - top).astype(BF)
        mixed = jnp.dot(turned[...], weights, preferred_element_type=F32)
        total = mixed[HEAD_DIM : HEAD_DIM + 1]
        span = slice(i * TILE, i * TILE + TILE)
        outs[b][:HEAD_DIM, span] = (mixed[:HEAD_DIM] / total).astype(BF)
        outs[b][HEAD_DIM:, span] = write_rim(top + jnp.log2(total)).astype(BF)

    score(0, even)
    for t in range(len(tiles)):
        here, there = (even, odd) if t % 2 == 0 else (odd, even)
        if t + 1 < len(tiles):
            score(t + 1, there)
        gather(t, here)


def attend(shifts, queries, pairs, turned, block):
    rows = pairs.shape[0]
    outs = [jax.ShapeDtypeStruct((ROWS, block), BF) for _ in shifts]
    work = len(shifts) * block * rows
    return call(
        functools.partial(attend_body, shifts),
        (queries, pairs, turned),
        outs,
        "attend",
        scratch=[pltpu.VMEM((rows, TILE), F32)] * 2,
        room=40,
        flops=work * 32,
    )


def merge(parts):
    logs = [jnp.sum(p[HEAD_DIM:].astype(F32), axis=0, keepdims=True) for p in parts]
    top = functools.reduce(jnp.maximum, logs)
    shares = [jnp.exp2(l - top) for l in logs]
    total = functools.reduce(jnp.add, shares)
    mixed = functools.reduce(
        jnp.add, [p[:HEAD_DIM].astype(F32) * s for p, s in zip(parts, shares)]
    )
    return mixed / total, top + jnp.log2(total)


def merge_body(*refs):
    ins, out = refs[:-1], refs[-1]
    width = out.shape[2]
    for i in range(out.shape[0]):
        mixed, lse = merge([r[:, i * width : i * width + width] for r in ins])
        out[i, :HEAD_DIM] = mixed
        out[i, HEAD_DIM:] = jnp.broadcast_to(lse, (FLAT, width))


def merge_flat(parts):
    logs = [p[HEAD_DIM : HEAD_DIM + 1] for p in parts]
    top = functools.reduce(jnp.maximum, logs)
    shares = [jnp.exp2(l - top) for l in logs]
    mixed = functools.reduce(jnp.add, [p[:HEAD_DIM] * s for p, s in zip(parts, shares)])
    return mixed / functools.reduce(jnp.add, shares)


def last_body(ins, out):
    heads = [merge_flat([ins[a * B + b] for a in range(A)]) for b in range(B)]
    out[...] = jnp.concatenate(heads, axis=0).T.astype(BF)


def step(part, shift):
    return lax.ppermute(part, "y", [(i, (i + shift) % Y) for i in range(Y)])


def local(queries, keys, values):
    count = queries.shape[0]
    block = count // Y
    ranks = lax.axis_size("head") * B
    tokens = keys.shape[0]
    sent = call(pack_body, (keys, values), jax.ShapeDtypeStruct((ranks, tokens, 128), BF), "pack")
    pairs = lax.all_to_all(sent, ("b", "head"), 0, 0, tiled=True).reshape(ranks * tokens, 128)
    columns = call(turn_body, (queries,), jax.ShapeDtypeStruct((128, count), BF), "turn")
    turned = call(prep_body, (pairs,), jax.ShapeDtypeStruct((ROWS, ranks * tokens), BF), "prep")
    far = attend((2,), columns, pairs, turned, block)[0]
    far = step(far, 1)
    right = attend((1,), columns, pairs, turned, block)[0]
    columns, far = lax.optimization_barrier((columns, far))
    right, far = step(right, 1), step(far, 1)
    left = attend((3,), columns, pairs, turned, block)[0]
    columns, right, far = lax.optimization_barrier((columns, right, far))
    left = step(left, 3)
    own = attend((0,), columns, pairs, turned, block)[0]
    width = block // (A * B)
    pieces = call(
        merge_body,
        (own, right, far, left),
        jax.ShapeDtypeStruct((A * B, HEAD_DIM + FLAT, width), F32),
        "merge",
    )
    pieces = lax.all_to_all(pieces, ("a", "b"), 0, 0, tiled=True)
    return call(last_body, (pieces,), jax.ShapeDtypeStruct((width, 128), BF), "last")


def solution(mesh):
    fine = Mesh(mesh.devices.reshape(Y, A, B, -1), ("y", "a", "b", "head"))
    frame = ("y", "a", "b")
    placed = (P(None, "head"), P((*frame, "head"), None), P((*frame, "head"), None))
    return jax.shard_map(
        local, mesh=fine, in_specs=placed, out_specs=P(frame, "head"), check_vma=False
    )
```

```python
import functools

import jax
import jax.numpy as jnp
from jax import lax
from jax.experimental import pallas as pl
from jax.experimental.pallas import tpu as pltpu
from jax.sharding import Mesh
from jax.sharding import PartitionSpec as P

HEAD_DIM = 64
RIM = 16
FLAT = 8
ROWS = HEAD_DIM + RIM
SCALE = 1.4426950408889634 * HEAD_DIM ** (-0.5)
Y, A, B = 4, 4, 2
TILE = 512
RUN = 1024
NARROW = 256
SAFE = 60.0
BF = jnp.bfloat16
F32 = jnp.float32
VMEM = pl.BlockSpec(memory_space=pltpu.VMEM)
LENGTHS = jax.ShapeDtypeStruct((1, TILE), F32)


def call(body, inputs, outs, name, scratch=(), room=16, flops=0):
    return pl.pallas_call(
        body,
        out_shape=outs,
        in_specs=[VMEM] * len(inputs),
        out_specs=jax.tree.map(lambda _: VMEM, outs),
        scratch_shapes=list(scratch),
        name=name,
        compiler_params=pltpu.CompilerParams(vmem_limit_bytes=room << 20),
        cost_estimate=pl.CostEstimate(flops=flops, transcendentals=0, bytes_accessed=1 << 18),
    )(*inputs)


def pack_body(keys, values, out):
    ranks = out.shape[0] // 2
    for j in range(ranks):
        k = keys[:, 128 * j : 128 * j + 128]
        v = values[:, 128 * j : 128 * j + 128]
        out[j] = jnp.concatenate([k[:, :HEAD_DIM], v[:, :HEAD_DIM]], axis=1)
        out[ranks + j] = jnp.concatenate([k[:, HEAD_DIM:], v[:, HEAD_DIM:]], axis=1)


def turn_body(queries, out, lengths):
    count = queries.shape[0]
    second = lax.axis_index("b") == 1
    out[HEAD_DIM:] = jnp.zeros((HEAD_DIM, count), BF)
    squares = []
    for i in range(0, count, TILE):
        t = queries[i : i + TILE, :].T
        own = jnp.where(second, t[HEAD_DIM:], t[:HEAD_DIM])
        out[:HEAD_DIM, i : i + TILE] = own
        squares.append(square_columns(own))
    lengths[...] = functools.reduce(jnp.maximum, squares)


def square_columns(columns):
    wide = columns.astype(F32)
    return jnp.sum(wide * wide, axis=0, keepdims=True)


def prep_body(pairs, out, lengths):
    squares = []
    for i in range(0, pairs.shape[0], TILE):
        t = pairs[i : i + TILE, :].T
        out[:HEAD_DIM, i : i + TILE] = t[HEAD_DIM:]
        squares.append(square_columns(t[:HEAD_DIM]))
    out[HEAD_DIM:] = jnp.ones((RIM, pairs.shape[0]), BF)
    lengths[...] = functools.reduce(jnp.maximum, squares)


def write_rim(lse):
    high = lse.astype(BF).astype(F32)
    rest = lse - high
    mid = rest.astype(BF).astype(F32)
    low = rest - mid
    row = lax.broadcasted_iota(jnp.int32, (RIM, lse.shape[1]), 0)
    return jnp.where(row == 0, high, jnp.where(row == 1, mid, jnp.where(row == 2, low, 0.0)))


def attend_body(shift, queries, pairs, turned, query_lengths, key_lengths, out, held):
    block = out.shape[1]
    tokens = pairs.shape[0]
    start = lax.rem(lax.axis_index("y") + shift, Y) * block

    def finish(mixed, top, span):
        total = mixed[HEAD_DIM : HEAD_DIM + 1]
        out[:HEAD_DIM, span] = (mixed[:HEAD_DIM] / total).astype(BF)
        out[HEAD_DIM:, span] = write_rim(top + jnp.log2(total)).astype(BF)

    bound = jnp.max(query_lengths[...]) * jnp.max(key_lengths[...]) * SCALE**2
    safe = bound <= SAFE**2

    @pl.when(safe)
    def _():
        columns = queries[:, pl.ds(pl.multiple_of(start, block), block)]
        mixed = None
        for r in range(0, tokens, RUN):
            scores = jnp.dot(pairs[r : r + RUN], columns, preferred_element_type=F32)
            weights = jnp.exp2(scores * SCALE).astype(BF)
            more = jnp.dot(turned[:, r : r + RUN], weights, preferred_element_type=F32)
            mixed = more if mixed is None else mixed + more
        finish(mixed, 0.0, slice(None))

    @pl.when(jnp.logical_not(safe))
    def _():
        @pl.loop(0, block // NARROW)
        def _(i):
            first = pl.multiple_of(start + i * NARROW, NARROW)
            held[...] = jnp.dot(
                pairs[...], queries[:, pl.ds(first, NARROW)], preferred_element_type=F32
            )
            top = jnp.max(held[...], axis=0, keepdims=True) * SCALE
            weights = jnp.exp2(held[...] * SCALE - top).astype(BF)
            mixed = jnp.dot(turned[...], weights, preferred_element_type=F32)
            finish(mixed, top, pl.ds(pl.multiple_of(i * NARROW, NARROW), NARROW))


def attend(shift, queries, pairs, turned, lengths, block):
    tokens = pairs.shape[0]
    return call(
        functools.partial(attend_body, shift),
        (queries, pairs, turned, *lengths),
        jax.ShapeDtypeStruct((ROWS, block), BF),
        "attend",
        scratch=[pltpu.VMEM((tokens, NARROW), F32)],
        room=40,
        flops=block * tokens * 32,
    )


def merge(parts):
    logs = [jnp.sum(p[HEAD_DIM:].astype(F32), axis=0, keepdims=True) for p in parts]
    top = functools.reduce(jnp.maximum, logs)
    shares = [jnp.exp2(l - top) for l in logs]
    total = functools.reduce(jnp.add, shares)
    mixed = functools.reduce(
        jnp.add, [p[:HEAD_DIM].astype(F32) * s for p, s in zip(parts, shares)]
    )
    return mixed / total, top + jnp.log2(total)


def merge_body(*refs):
    ins, out = refs[:-1], refs[-1]
    width = out.shape[2]
    for i in range(out.shape[0]):
        mixed, lse = merge([r[:, i * width : i * width + width] for r in ins])
        out[i, :HEAD_DIM] = mixed
        out[i, HEAD_DIM:] = jnp.broadcast_to(lse, (FLAT, width))


def merge_flat(parts):
    logs = [p[HEAD_DIM : HEAD_DIM + 1] for p in parts]
    top = functools.reduce(jnp.maximum, logs)
    shares = [jnp.exp2(l - top) for l in logs]
    mixed = functools.reduce(jnp.add, [p[:HEAD_DIM] * s for p, s in zip(parts, shares)])
    return mixed / functools.reduce(jnp.add, shares)


def last_body(ins, out):
    heads = [merge_flat([ins[a * B + b] for a in range(A)]) for b in range(B)]
    out[...] = jnp.concatenate(heads, axis=0).T.astype(BF)


def step(part, shift):
    return lax.ppermute(part, "y", [(i, (i + shift) % Y) for i in range(Y)])


def local(queries, keys, values):
    count = queries.shape[0]
    block = count // Y
    ranks = lax.axis_size("head") * B
    tokens = keys.shape[0]
    sent = call(pack_body, (keys, values), jax.ShapeDtypeStruct((ranks, tokens, 128), BF), "pack")
    pairs = lax.all_to_all(sent, ("b", "head"), 0, 0, tiled=True).reshape(ranks * tokens, 128)
    columns, query_lengths = call(
        turn_body, (queries,), (jax.ShapeDtypeStruct((128, count), BF), LENGTHS), "turn"
    )
    turned, key_lengths = call(
        prep_body,
        (pairs,),
        (jax.ShapeDtypeStruct((ROWS, ranks * tokens), BF), LENGTHS),
        "prep",
    )
    lengths = (query_lengths, key_lengths)
    far = attend(2, columns, pairs, turned, lengths, block)
    far = step(far, 1)
    right = attend(1, columns, pairs, turned, lengths, block)
    columns, far = lax.optimization_barrier((columns, far))
    right, far = step(right, 1), step(far, 1)
    left = attend(3, columns, pairs, turned, lengths, block)
    columns, right, far = lax.optimization_barrier((columns, right, far))
    left = step(left, 3)
    own = attend(0, columns, pairs, turned, lengths, block)
    width = block // (A * B)
    pieces = call(
        merge_body,
        (own, right, far, left),
        jax.ShapeDtypeStruct((A * B, HEAD_DIM + FLAT, width), F32),
        "merge",
    )
    pieces = lax.all_to_all(pieces, ("a", "b"), 0, 0, tiled=True)
    return call(last_body, (pieces,), jax.ShapeDtypeStruct((width, 128), BF), "last")


def solution(mesh):
    fine = Mesh(mesh.devices.reshape(Y, A, B, -1), ("y", "a", "b", "head"))
    frame = ("y", "a", "b")
    placed = (P(None, "head"), P((*frame, "head"), None), P((*frame, "head"), None))
    return jax.shard_map(
        local, mesh=fine, in_specs=placed, out_specs=P(frame, "head"), check_vma=False
    )
```

```python
import functools

import jax
import jax.numpy as jnp
from jax import lax
from jax.experimental import pallas as pl
from jax.experimental.pallas import tpu as pltpu
from jax.sharding import Mesh
from jax.sharding import PartitionSpec as P

HEAD_DIM = 64
RIM = 16
FLAT = 8
ROWS = HEAD_DIM + RIM
SCALE = 1.4426950408889634 * HEAD_DIM ** (-0.5)
Y, A, B = 4, 4, 2
TILE = 512
PACKS = 2
RUN = 1024
NARROW = 256
SAFE = 60.0
BF = jnp.bfloat16
F32 = jnp.float32
VMEM = pl.BlockSpec(memory_space=pltpu.VMEM)
LENGTHS = jax.ShapeDtypeStruct((1, TILE), F32)


def call(body, inputs, outs, name, scratch=(), room=16, flops=0):
    return pl.pallas_call(
        body,
        out_shape=outs,
        in_specs=[VMEM] * len(inputs),
        out_specs=jax.tree.map(lambda _: VMEM, outs),
        scratch_shapes=list(scratch),
        name=name,
        compiler_params=pltpu.CompilerParams(vmem_limit_bytes=room << 20),
        cost_estimate=pl.CostEstimate(flops=flops, transcendentals=0, bytes_accessed=1 << 18),
    )(*inputs)


def pack_body(keys, values, out):
    ranks = out.shape[0] // 2
    for j in range(ranks):
        k = keys[:, 128 * j : 128 * j + 128]
        v = values[:, 128 * j : 128 * j + 128]
        out[j] = jnp.concatenate([k[:, :HEAD_DIM], v[:, :HEAD_DIM]], axis=1)
        out[ranks + j] = jnp.concatenate([k[:, HEAD_DIM:], v[:, HEAD_DIM:]], axis=1)


def turn_body(queries, out, lengths):
    count = queries.shape[0]
    second = lax.axis_index("b") == 1
    out[HEAD_DIM:] = jnp.zeros((HEAD_DIM, count), BF)
    squares = []
    for i in range(0, count, TILE):
        t = queries[i : i + TILE, :].T
        own = jnp.where(second, t[HEAD_DIM:], t[:HEAD_DIM])
        out[:HEAD_DIM, i : i + TILE] = own
        squares.append(square_columns(own))
    lengths[...] = functools.reduce(jnp.maximum, squares)


def square_columns(columns):
    wide = columns.astype(F32)
    return jnp.sum(wide * wide, axis=0, keepdims=True)


def prep_body(pairs, out, lengths):
    squares = []
    for i in range(0, pairs.shape[0], TILE):
        t = pairs[i : i + TILE, :].T
        out[:HEAD_DIM, i : i + TILE] = t[HEAD_DIM:]
        squares.append(square_columns(t[:HEAD_DIM]))
    out[HEAD_DIM:] = jnp.ones((RIM, pairs.shape[0]), BF)
    lengths[...] = functools.reduce(jnp.maximum, squares)


def write_rim(lse):
    high = lse.astype(BF).astype(F32)
    rest = lse - high
    mid = rest.astype(BF).astype(F32)
    low = rest - mid
    row = lax.broadcasted_iota(jnp.int32, (RIM, lse.shape[1]), 0)
    return jnp.where(row == 0, high, jnp.where(row == 1, mid, jnp.where(row == 2, low, 0.0)))


def attend_body(shift, queries, pairs, turned, query_lengths, key_lengths, out, held):
    block = out.shape[1]
    tokens = pairs.shape[0]
    start = lax.rem(lax.axis_index("y") + shift, Y) * block

    def finish(mixed, top, span):
        total = mixed[HEAD_DIM : HEAD_DIM + 1]
        out[:HEAD_DIM, span] = (mixed[:HEAD_DIM] / total).astype(BF)
        out[HEAD_DIM:, span] = write_rim(top + jnp.log2(total)).astype(BF)

    bound = jnp.max(query_lengths[...]) * jnp.max(key_lengths[...]) * SCALE**2
    safe = bound <= SAFE**2

    @pl.when(safe)
    def _():
        columns = queries[:, pl.ds(pl.multiple_of(start, block), block)]
        mixed = None
        for r in range(0, tokens, RUN):
            scores = jnp.dot(pairs[r : r + RUN], columns, preferred_element_type=F32)
            weights = jnp.exp2(scores * SCALE).astype(BF)
            more = jnp.dot(turned[:, r : r + RUN], weights, preferred_element_type=F32)
            mixed = more if mixed is None else mixed + more
        finish(mixed, 0.0, slice(None))

    @pl.when(jnp.logical_not(safe))
    def _():
        @pl.loop(0, block // NARROW)
        def _(i):
            first = pl.multiple_of(start + i * NARROW, NARROW)
            held[...] = jnp.dot(
                pairs[...], queries[:, pl.ds(first, NARROW)], preferred_element_type=F32
            )
            top = jnp.max(held[...], axis=0, keepdims=True) * SCALE
            weights = jnp.exp2(held[...] * SCALE - top).astype(BF)
            mixed = jnp.dot(turned[...], weights, preferred_element_type=F32)
            finish(mixed, top, pl.ds(pl.multiple_of(i * NARROW, NARROW), NARROW))


def attend(shift, queries, pairs, turned, lengths, block):
    tokens = pairs.shape[0]
    return call(
        functools.partial(attend_body, shift),
        (queries, pairs, turned, *lengths),
        jax.ShapeDtypeStruct((ROWS, block), BF),
        "attend",
        scratch=[pltpu.VMEM((tokens, NARROW), F32)],
        room=40,
        flops=block * tokens * 32,
    )


def merge(parts):
    logs = [jnp.sum(p[HEAD_DIM:].astype(F32), axis=0, keepdims=True) for p in parts]
    top = functools.reduce(jnp.maximum, logs)
    shares = [jnp.exp2(l - top) for l in logs]
    total = functools.reduce(jnp.add, shares)
    mixed = functools.reduce(
        jnp.add, [p[:HEAD_DIM].astype(F32) * s for p, s in zip(parts, shares)]
    )
    return mixed / total, top + jnp.log2(total)


def merge_body(*refs):
    ins, out = refs[:-1], refs[-1]
    width = out.shape[2]
    for i in range(out.shape[0]):
        mixed, lse = merge([r[:, i * width : i * width + width] for r in ins])
        out[i, :HEAD_DIM] = mixed
        out[i, HEAD_DIM:] = jnp.broadcast_to(lse, (FLAT, width))


def join_body(mine, passing, out):
    mixed, lse = merge([mine[...], passing[...]])
    out[:HEAD_DIM] = mixed.astype(BF)
    out[HEAD_DIM:] = write_rim(lse).astype(BF)


def merge_flat(parts):
    logs = [p[HEAD_DIM : HEAD_DIM + 1] for p in parts]
    top = functools.reduce(jnp.maximum, logs)
    shares = [jnp.exp2(l - top) for l in logs]
    mixed = functools.reduce(jnp.add, [p[:HEAD_DIM] * s for p, s in zip(parts, shares)])
    return mixed / functools.reduce(jnp.add, shares)


def last_body(ins, out):
    heads = [merge_flat([ins[a * B + b] for a in range(A)]) for b in range(B)]
    out[...] = jnp.concatenate(heads, axis=0).T.astype(BF)


def step(part, shift):
    return lax.ppermute(part, "y", [(i, (i + shift) % Y) for i in range(Y)])


def local(queries, keys, values):
    count = queries.shape[0]
    block = count // Y
    ranks = lax.axis_size("head") * B
    tokens = keys.shape[0]
    part = tokens // PACKS
    sent = pl.pallas_call(
        pack_body,
        grid=(PACKS,),
        in_specs=[pl.BlockSpec((part, keys.shape[1]), lambda i: (i, 0))] * 2,
        out_specs=pl.BlockSpec((ranks, part, 128), lambda i: (0, i, 0)),
        out_shape=jax.ShapeDtypeStruct((ranks, tokens, 128), BF),
        name="pack",
    )(keys, values)
    pairs = lax.all_to_all(sent, ("b", "head"), 0, 0, tiled=True).reshape(ranks * tokens, 128)
    columns, query_lengths = call(
        turn_body, (queries,), (jax.ShapeDtypeStruct((128, count), BF), LENGTHS), "turn"
    )
    turned, key_lengths = call(
        prep_body,
        (pairs,),
        (jax.ShapeDtypeStruct((ROWS, ranks * tokens), BF), LENGTHS),
        "prep",
    )
    lengths = (query_lengths, key_lengths)
    far = step(attend(2, columns, pairs, turned, lengths, block), 1)
    right = attend(1, columns, pairs, turned, lengths, block)
    right = call(join_body, (right, far), jax.ShapeDtypeStruct((ROWS, block), BF), "join")
    columns, right = lax.optimization_barrier((columns, right))
    left = attend(3, columns, pairs, turned, lengths, block)
    right = step(right, 1)
    columns, right = lax.optimization_barrier((columns, right))
    left = step(left, 3)
    own = attend(0, columns, pairs, turned, lengths, block)
    width = block // (A * B)
    pieces = call(
        merge_body,
        (own, right, left),
        jax.ShapeDtypeStruct((A * B, HEAD_DIM + FLAT, width), F32),
        "merge",
    )
    pieces = lax.all_to_all(pieces, ("a", "b"), 0, 0, tiled=True)
    return call(last_body, (pieces,), jax.ShapeDtypeStruct((width, 128), BF), "last")


def solution(mesh):
    fine = Mesh(mesh.devices.reshape(Y, A, B, -1), ("y", "a", "b", "head"))
    frame = ("y", "a", "b")
    placed = (P(None, "head"), P((*frame, "head"), None), P((*frame, "head"), None))
    return jax.shard_map(
        local, mesh=fine, in_specs=placed, out_specs=P(frame, "head"), check_vma=False
    )
```

```python
import functools

import jax
import jax.numpy as jnp
from jax import lax
from jax.experimental import pallas as pl
from jax.experimental.pallas import tpu as pltpu
from jax.sharding import Mesh
from jax.sharding import PartitionSpec as P

HEAD_DIM = 64
RIM = 16
ROWS = HEAD_DIM + RIM
SCALE = 1.4426950408889634 * HEAD_DIM ** (-0.5)
Y, A, B = 4, 4, 2
TILE = 512
PACKS = 2
RUN = 1024
NARROW = 256
SAFE = 60.0
BF = jnp.bfloat16
F32 = jnp.float32
VMEM = pl.BlockSpec(memory_space=pltpu.VMEM)
LENGTHS = jax.ShapeDtypeStruct((1, TILE), F32)


def call(body, inputs, outs, name, scratch=(), room=16, flops=0):
    return pl.pallas_call(
        body,
        out_shape=outs,
        in_specs=[VMEM] * len(inputs),
        out_specs=jax.tree.map(lambda _: VMEM, outs),
        scratch_shapes=list(scratch),
        name=name,
        compiler_params=pltpu.CompilerParams(vmem_limit_bytes=room << 20),
        cost_estimate=pl.CostEstimate(flops=flops, transcendentals=0, bytes_accessed=1 << 18),
    )(*inputs)


def pack_body(keys, values, out):
    ranks = out.shape[0] // 2
    for j in range(ranks):
        k = keys[:, 128 * j : 128 * j + 128]
        v = values[:, 128 * j : 128 * j + 128]
        out[j] = jnp.concatenate([k[:, :HEAD_DIM], v[:, :HEAD_DIM]], axis=1)
        out[ranks + j] = jnp.concatenate([k[:, HEAD_DIM:], v[:, HEAD_DIM:]], axis=1)


def turn_body(queries, out, lengths):
    count = queries.shape[0]
    second = lax.axis_index("b") == 1
    out[HEAD_DIM:] = jnp.zeros((HEAD_DIM, count), BF)
    squares = []
    for i in range(0, count, TILE):
        t = queries[i : i + TILE, :].T
        own = jnp.where(second, t[HEAD_DIM:], t[:HEAD_DIM])
        out[:HEAD_DIM, i : i + TILE] = own
        squares.append(square_columns(own))
    lengths[...] = functools.reduce(jnp.maximum, squares)


def square_columns(columns):
    wide = columns.astype(F32)
    return jnp.sum(wide * wide, axis=0, keepdims=True)


def prep_body(pairs, out, lengths):
    squares = []
    for i in range(0, pairs.shape[0], TILE):
        t = pairs[i : i + TILE, :].T
        out[:HEAD_DIM, i : i + TILE] = t[HEAD_DIM:]
        squares.append(square_columns(t[:HEAD_DIM]))
    out[HEAD_DIM:] = jnp.ones((RIM, pairs.shape[0]), BF)
    lengths[...] = functools.reduce(jnp.maximum, squares)


def write_rim(lse):
    high = lse.astype(BF).astype(F32)
    rest = lse - high
    mid = rest.astype(BF).astype(F32)
    low = rest - mid
    row = lax.broadcasted_iota(jnp.int32, (RIM, lse.shape[1]), 0)
    return jnp.where(row == 0, high, jnp.where(row == 1, mid, jnp.where(row == 2, low, 0.0)))


def attend_body(shift, queries, pairs, turned, query_lengths, key_lengths, out, held):
    block = out.shape[1]
    tokens = pairs.shape[0]
    start = lax.rem(lax.axis_index("y") + shift, Y) * block

    def finish(mixed, top, span):
        total = mixed[HEAD_DIM : HEAD_DIM + 1]
        out[:HEAD_DIM, span] = (mixed[:HEAD_DIM] / total).astype(BF)
        out[HEAD_DIM:, span] = write_rim(top + jnp.log2(total)).astype(BF)

    bound = jnp.max(query_lengths[...]) * jnp.max(key_lengths[...]) * SCALE**2
    safe = bound <= SAFE**2

    @pl.when(safe)
    def _():
        columns = queries[:, pl.ds(pl.multiple_of(start, block), block)]
        mixed = None
        for r in range(0, tokens, RUN):
            scores = jnp.dot(pairs[r : r + RUN], columns, preferred_element_type=F32)
            weights = jnp.exp2(scores * SCALE).astype(BF)
            more = jnp.dot(turned[:, r : r + RUN], weights, preferred_element_type=F32)
            mixed = more if mixed is None else mixed + more
        finish(mixed, 0.0, slice(None))

    @pl.when(jnp.logical_not(safe))
    def _():
        @pl.loop(0, block // NARROW)
        def _(i):
            first = pl.multiple_of(start + i * NARROW, NARROW)
            held[...] = jnp.dot(
                pairs[...], queries[:, pl.ds(first, NARROW)], preferred_element_type=F32
            )
            top = jnp.max(held[...], axis=0, keepdims=True) * SCALE
            weights = jnp.exp2(held[...] * SCALE - top).astype(BF)
            mixed = jnp.dot(turned[...], weights, preferred_element_type=F32)
            finish(mixed, top, pl.ds(pl.multiple_of(i * NARROW, NARROW), NARROW))


def attend(shift, queries, pairs, turned, lengths, block):
    tokens = pairs.shape[0]
    return call(
        functools.partial(attend_body, shift),
        (queries, pairs, turned, *lengths),
        jax.ShapeDtypeStruct((ROWS, block), BF),
        "attend",
        scratch=[pltpu.VMEM((tokens, NARROW), F32)],
        room=40,
        flops=block * tokens * 32,
    )


def merge(parts):
    logs = [jnp.sum(p[HEAD_DIM:].astype(F32), axis=0, keepdims=True) for p in parts]
    top = functools.reduce(jnp.maximum, logs)
    shares = [jnp.exp2(l - top) for l in logs]
    total = functools.reduce(jnp.add, shares)
    mixed = functools.reduce(
        jnp.add, [p[:HEAD_DIM].astype(F32) * s for p, s in zip(parts, shares)]
    )
    return mixed / total, top + jnp.log2(total)


def merge_body(*refs):
    ins, out = refs[:-1], refs[-1]
    width = out.shape[2]
    for i in range(out.shape[0]):
        mixed, lse = merge([r[:, i * width : i * width + width] for r in ins])
        out[i, :HEAD_DIM] = mixed.astype(BF)
        out[i, HEAD_DIM:] = write_rim(lse).astype(BF)


def join_body(mine, passing, out):
    mixed, lse = merge([mine[...], passing[...]])
    out[:HEAD_DIM] = mixed.astype(BF)
    out[HEAD_DIM:] = write_rim(lse).astype(BF)


def last_body(ins, out):
    heads = [merge([ins[a * B + b] for a in range(A)])[0] for b in range(B)]
    out[...] = jnp.concatenate(heads, axis=0).T.astype(BF)


def step(part, shift):
    return lax.ppermute(part, "y", [(i, (i + shift) % Y) for i in range(Y)])


def local(queries, keys, values):
    count = queries.shape[0]
    block = count // Y
    ranks = lax.axis_size("head") * B
    tokens = keys.shape[0]
    part = tokens // PACKS
    sent = pl.pallas_call(
        pack_body,
        grid=(PACKS,),
        in_specs=[pl.BlockSpec((part, keys.shape[1]), lambda i: (i, 0))] * 2,
        out_specs=pl.BlockSpec((ranks, part, 128), lambda i: (0, i, 0)),
        out_shape=jax.ShapeDtypeStruct((ranks, tokens, 128), BF),
        name="pack",
    )(keys, values)
    pairs = lax.all_to_all(sent, ("b", "head"), 0, 0, tiled=True).reshape(ranks * tokens, 128)
    columns, query_lengths = call(
        turn_body, (queries,), (jax.ShapeDtypeStruct((128, count), BF), LENGTHS), "turn"
    )
    turned, key_lengths = call(
        prep_body,
        (pairs,),
        (jax.ShapeDtypeStruct((ROWS, ranks * tokens), BF), LENGTHS),
        "prep",
    )
    lengths = (query_lengths, key_lengths)
    far = step(attend(2, columns, pairs, turned, lengths, block), 1)
    right = attend(1, columns, pairs, turned, lengths, block)
    right = call(join_body, (right, far), jax.ShapeDtypeStruct((ROWS, block), BF), "join")
    columns, right = lax.optimization_barrier((columns, right))
    left = attend(3, columns, pairs, turned, lengths, block)
    right = step(right, 1)
    columns, right = lax.optimization_barrier((columns, right))
    left = step(left, 3)
    own = attend(0, columns, pairs, turned, lengths, block)
    width = block // (A * B)
    pieces = call(
        merge_body,
        (own, right, left),
        jax.ShapeDtypeStruct((A * B, ROWS, width), BF),
        "merge",
    )
    pieces = lax.all_to_all(pieces, ("a", "b"), 0, 0, tiled=True)
    return call(last_body, (pieces,), jax.ShapeDtypeStruct((width, 128), BF), "last")


def solution(mesh):
    fine = Mesh(mesh.devices.reshape(Y, A, B, -1), ("y", "a", "b", "head"))
    frame = ("y", "a", "b")
    placed = (P(None, "head"), P((*frame, "head"), None), P((*frame, "head"), None))
    return jax.shard_map(
        local, mesh=fine, in_specs=placed, out_specs=P(frame, "head"), check_vma=False
    )
```

```python
import functools

import jax
import jax.numpy as jnp
from jax import lax
from jax.experimental import pallas as pl
from jax.experimental.pallas import tpu as pltpu
from jax.sharding import Mesh
from jax.sharding import PartitionSpec as P

HEAD_DIM = 64
RIM = 8
ROWS = HEAD_DIM + RIM
SCALE = 1.4426950408889634 * HEAD_DIM ** (-0.5)
Y, A, B = 4, 4, 2
TILE = 512
PACKS = 2
RUN = 1024
NARROW = 256
SAFE = 60.0
BF = jnp.bfloat16
F32 = jnp.float32
VMEM = pl.BlockSpec(memory_space=pltpu.VMEM)
LENGTHS = jax.ShapeDtypeStruct((1, TILE), F32)


def call(body, inputs, outs, name, scratch=(), room=16, flops=0):
    return pl.pallas_call(
        body,
        out_shape=outs,
        in_specs=[VMEM] * len(inputs),
        out_specs=jax.tree.map(lambda _: VMEM, outs),
        scratch_shapes=list(scratch),
        name=name,
        compiler_params=pltpu.CompilerParams(vmem_limit_bytes=room << 20),
        cost_estimate=pl.CostEstimate(flops=flops, transcendentals=0, bytes_accessed=1 << 18),
    )(*inputs)


def pack_body(keys, values, out):
    ranks = out.shape[0] // 2
    for j in range(ranks):
        k = keys[:, 128 * j : 128 * j + 128]
        v = values[:, 128 * j : 128 * j + 128]
        out[j] = jnp.concatenate([k[:, :HEAD_DIM], v[:, :HEAD_DIM]], axis=1)
        out[ranks + j] = jnp.concatenate([k[:, HEAD_DIM:], v[:, HEAD_DIM:]], axis=1)


def turn_body(queries, out, lengths):
    count = queries.shape[0]
    second = lax.axis_index("b") == 1
    out[HEAD_DIM:] = jnp.zeros((HEAD_DIM, count), BF)
    squares = []
    for i in range(0, count, TILE):
        t = queries[i : i + TILE, :].T
        own = jnp.where(second, t[HEAD_DIM:], t[:HEAD_DIM])
        out[:HEAD_DIM, i : i + TILE] = own
        squares.append(square_columns(own))
    lengths[...] = functools.reduce(jnp.maximum, squares)


def square_columns(columns):
    wide = columns.astype(F32)
    return jnp.sum(wide * wide, axis=0, keepdims=True)


def prep_body(pairs, out, lengths):
    squares = []
    for i in range(0, pairs.shape[0], TILE):
        t = pairs[i : i + TILE, :].T
        out[:HEAD_DIM, i : i + TILE] = t[HEAD_DIM:]
        squares.append(square_columns(t[:HEAD_DIM]))
    out[HEAD_DIM:] = jnp.ones((RIM, pairs.shape[0]), BF)
    lengths[...] = functools.reduce(jnp.maximum, squares)


def write_rim(lse):
    high = lse.astype(BF).astype(F32)
    rest = lse - high
    mid = rest.astype(BF).astype(F32)
    low = rest - mid
    row = lax.broadcasted_iota(jnp.int32, (RIM, lse.shape[1]), 0)
    return jnp.where(row == 0, high, jnp.where(row == 1, mid, jnp.where(row == 2, low, 0.0)))


def attend_body(shift, queries, pairs, turned, query_lengths, key_lengths, out, held):
    block = out.shape[1]
    tokens = pairs.shape[0]
    start = lax.rem(lax.axis_index("y") + shift, Y) * block

    def finish(mixed, top, span):
        total = mixed[HEAD_DIM : HEAD_DIM + 1]
        out[:HEAD_DIM, span] = (mixed[:HEAD_DIM] / total).astype(BF)
        out[HEAD_DIM:, span] = write_rim(top + jnp.log2(total)).astype(BF)

    bound = jnp.max(query_lengths[...]) * jnp.max(key_lengths[...]) * SCALE**2
    safe = bound <= SAFE**2

    @pl.when(safe)
    def _():
        columns = queries[:, pl.ds(pl.multiple_of(start, block), block)]
        mixed = None
        for r in range(0, tokens, RUN):
            scores = jnp.dot(pairs[r : r + RUN], columns, preferred_element_type=F32)
            weights = jnp.exp2(scores * SCALE).astype(BF)
            more = jnp.dot(turned[:, r : r + RUN], weights, preferred_element_type=F32)
            mixed = more if mixed is None else mixed + more
        finish(mixed, 0.0, slice(None))

    @pl.when(jnp.logical_not(safe))
    def _():
        @pl.loop(0, block // NARROW)
        def _(i):
            first = pl.multiple_of(start + i * NARROW, NARROW)
            held[...] = jnp.dot(
                pairs[...], queries[:, pl.ds(first, NARROW)], preferred_element_type=F32
            )
            top = jnp.max(held[...], axis=0, keepdims=True) * SCALE
            weights = jnp.exp2(held[...] * SCALE - top).astype(BF)
            mixed = jnp.dot(turned[...], weights, preferred_element_type=F32)
            finish(mixed, top, pl.ds(pl.multiple_of(i * NARROW, NARROW), NARROW))


def attend(shift, queries, pairs, turned, lengths, block):
    tokens = pairs.shape[0]
    return call(
        functools.partial(attend_body, shift),
        (queries, pairs, turned, *lengths),
        jax.ShapeDtypeStruct((ROWS, block), BF),
        "attend",
        scratch=[pltpu.VMEM((tokens, NARROW), F32)],
        room=40,
        flops=block * tokens * 32,
    )


def merge(parts):
    logs = [jnp.sum(p[HEAD_DIM:].astype(F32), axis=0, keepdims=True) for p in parts]
    top = functools.reduce(jnp.maximum, logs)
    shares = [jnp.exp2(l - top) for l in logs]
    total = functools.reduce(jnp.add, shares)
    mixed = functools.reduce(
        jnp.add, [p[:HEAD_DIM].astype(F32) * s for p, s in zip(parts, shares)]
    )
    return mixed / total, top + jnp.log2(total)


def merge_body(*refs):
    ins, out = refs[:-1], refs[-1]
    width = out.shape[2]
    for i in range(out.shape[0]):
        mixed, lse = merge([r[:, i * width : i * width + width] for r in ins])
        out[i, :HEAD_DIM] = mixed.astype(BF)
        out[i, HEAD_DIM:] = write_rim(lse).astype(BF)


def join_body(mine, passing, out):
    mixed, lse = merge([mine[...], passing[...]])
    out[:HEAD_DIM] = mixed.astype(BF)
    out[HEAD_DIM:] = write_rim(lse).astype(BF)


def last_body(ins, out):
    heads = [merge([ins[a * B + b] for a in range(A)])[0] for b in range(B)]
    out[...] = jnp.concatenate(heads, axis=0).T.astype(BF)


def step(part, shift):
    return lax.ppermute(part, "y", [(i, (i + shift) % Y) for i in range(Y)])


def local(queries, keys, values):
    count = queries.shape[0]
    block = count // Y
    ranks = lax.axis_size("head") * B
    tokens = keys.shape[0]
    part = tokens // PACKS
    sent = pl.pallas_call(
        pack_body,
        grid=(PACKS,),
        in_specs=[pl.BlockSpec((part, keys.shape[1]), lambda i: (i, 0))] * 2,
        out_specs=pl.BlockSpec((ranks, part, 128), lambda i: (0, i, 0)),
        out_shape=jax.ShapeDtypeStruct((ranks, tokens, 128), BF),
        name="pack",
    )(keys, values)
    pairs = lax.all_to_all(sent, ("b", "head"), 0, 0, tiled=True).reshape(ranks * tokens, 128)
    columns, query_lengths = call(
        turn_body, (queries,), (jax.ShapeDtypeStruct((128, count), BF), LENGTHS), "turn"
    )
    turned, key_lengths = call(
        prep_body,
        (pairs,),
        (jax.ShapeDtypeStruct((ROWS, ranks * tokens), BF), LENGTHS),
        "prep",
    )
    lengths = (query_lengths, key_lengths)
    far = step(attend(2, columns, pairs, turned, lengths, block), 1)
    right = attend(1, columns, pairs, turned, lengths, block)
    right = call(join_body, (right, far), jax.ShapeDtypeStruct((ROWS, block), BF), "join")
    columns, right = lax.optimization_barrier((columns, right))
    left = attend(3, columns, pairs, turned, lengths, block)
    right = step(right, 1)
    columns, right = lax.optimization_barrier((columns, right))
    left = step(left, 3)
    own = attend(0, columns, pairs, turned, lengths, block)
    width = block // (A * B)
    pieces = call(
        merge_body,
        (own, right, left),
        jax.ShapeDtypeStruct((A * B, ROWS, width), BF),
        "merge",
    )
    pieces = lax.all_to_all(pieces, ("a", "b"), 0, 0, tiled=True)
    return call(last_body, (pieces,), jax.ShapeDtypeStruct((width, 128), BF), "last")


def solution(mesh):
    fine = Mesh(mesh.devices.reshape(Y, A, B, -1), ("y", "a", "b", "head"))
    frame = ("y", "a", "b")
    placed = (P(None, "head"), P((*frame, "head"), None), P((*frame, "head"), None))
    return jax.shard_map(
        local, mesh=fine, in_specs=placed, out_specs=P(frame, "head"), check_vma=False
    )
```

```python
import functools

import jax
import jax.numpy as jnp
from jax import lax
from jax.experimental import pallas as pl
from jax.experimental.pallas import tpu as pltpu
from jax.sharding import Mesh
from jax.sharding import PartitionSpec as P

HEAD_DIM = 64
RIM = 8
ROWS = HEAD_DIM + RIM
SCALE = 1.4426950408889634 * HEAD_DIM ** (-0.5)
Y, A, B = 4, 4, 2
TILE = 512
PACKS = 2
RUN = 1024
NARROW = 256
SAFE = 60.0
BF = jnp.bfloat16
F32 = jnp.float32
VMEM = pl.BlockSpec(memory_space=pltpu.VMEM)
LENGTHS = jax.ShapeDtypeStruct((1, TILE), F32)


def call(body, inputs, outs, name, scratch=(), room=16, flops=0):
    return pl.pallas_call(
        body,
        out_shape=outs,
        in_specs=[VMEM] * len(inputs),
        out_specs=jax.tree.map(lambda _: VMEM, outs),
        scratch_shapes=list(scratch),
        name=name,
        compiler_params=pltpu.CompilerParams(vmem_limit_bytes=room << 20),
        cost_estimate=pl.CostEstimate(flops=flops, transcendentals=0, bytes_accessed=1 << 18),
    )(*inputs)


def pack_body(keys, values, out):
    ranks = out.shape[0] // 2
    for j in range(ranks):
        k = keys[:, 128 * j : 128 * j + 128]
        v = values[:, 128 * j : 128 * j + 128]
        out[j] = jnp.concatenate([k[:, :HEAD_DIM], v[:, :HEAD_DIM]], axis=1)
        out[ranks + j] = jnp.concatenate([k[:, HEAD_DIM:], v[:, HEAD_DIM:]], axis=1)


def turn_body(queries, out, lengths):
    count = queries.shape[0]
    second = lax.axis_index("b") == 1
    out[HEAD_DIM:] = jnp.zeros((HEAD_DIM, count), BF)
    squares = []
    for i in range(0, count, TILE):
        t = queries[i : i + TILE, :].T
        own = jnp.where(second, t[HEAD_DIM:], t[:HEAD_DIM])
        out[:HEAD_DIM, i : i + TILE] = own
        squares.append(square_columns(own))
    lengths[...] = functools.reduce(jnp.maximum, squares)


def square_columns(columns):
    wide = columns.astype(F32)
    return jnp.sum(wide * wide, axis=0, keepdims=True)


def prep_body(pairs, out, lengths):
    squares = []
    for i in range(0, pairs.shape[0], TILE):
        t = pairs[i : i + TILE, :].T
        out[:HEAD_DIM, i : i + TILE] = t[HEAD_DIM:]
        squares.append(square_columns(t[:HEAD_DIM]))
    out[HEAD_DIM:] = jnp.ones((RIM, pairs.shape[0]), BF)
    lengths[...] = functools.reduce(jnp.maximum, squares)


def write_rim(lse):
    high = lse.astype(BF).astype(F32)
    rest = lse - high
    mid = rest.astype(BF).astype(F32)
    low = rest - mid
    row = lax.broadcasted_iota(jnp.int32, (RIM, lse.shape[1]), 0)
    return jnp.where(row == 0, high, jnp.where(row == 1, mid, jnp.where(row == 2, low, 0.0)))


def attend_body(shift, queries, pairs, turned, query_lengths, key_lengths, out, held):
    block = out.shape[1]
    tokens = pairs.shape[0]
    start = lax.rem(lax.axis_index("y") + shift, Y) * block

    def finish(mixed, top, span):
        total = mixed[HEAD_DIM : HEAD_DIM + 1]
        out[:HEAD_DIM, span] = (mixed[:HEAD_DIM] / total).astype(BF)
        out[HEAD_DIM:, span] = write_rim(top + jnp.log2(total)).astype(BF)

    bound = jnp.max(query_lengths[...]) * jnp.max(key_lengths[...]) * SCALE**2
    safe = bound <= SAFE**2

    @pl.when(safe)
    def _():
        columns = queries[:, pl.ds(pl.multiple_of(start, block), block)]
        mixed = None
        for r in range(0, tokens, RUN):
            scores = jnp.dot(pairs[r : r + RUN], columns, preferred_element_type=F32)
            weights = jnp.exp2(scores * SCALE).astype(BF)
            more = jnp.dot(turned[:, r : r + RUN], weights, preferred_element_type=F32)
            mixed = more if mixed is None else mixed + more
        finish(mixed, 0.0, slice(None))

    @pl.when(jnp.logical_not(safe))
    def _():
        @pl.loop(0, block // NARROW)
        def _(i):
            first = pl.multiple_of(start + i * NARROW, NARROW)
            held[...] = jnp.dot(
                pairs[...], queries[:, pl.ds(first, NARROW)], preferred_element_type=F32
            )
            top = jnp.max(held[...], axis=0, keepdims=True) * SCALE
            weights = jnp.exp2(held[...] * SCALE - top).astype(BF)
            mixed = jnp.dot(turned[...], weights, preferred_element_type=F32)
            finish(mixed, top, pl.ds(pl.multiple_of(i * NARROW, NARROW), NARROW))


def attend(shift, queries, pairs, turned, lengths, block):
    tokens = pairs.shape[0]
    return call(
        functools.partial(attend_body, shift),
        (queries, pairs, turned, *lengths),
        jax.ShapeDtypeStruct((ROWS, block), BF),
        "attend",
        scratch=[pltpu.VMEM((tokens, NARROW), F32)],
        room=40,
        flops=block * tokens * 32,
    )


def merge(parts):
    logs = [jnp.sum(p[HEAD_DIM:].astype(F32), axis=0, keepdims=True) for p in parts]
    top = functools.reduce(jnp.maximum, logs)
    shares = [jnp.exp2(l - top) for l in logs]
    total = functools.reduce(jnp.add, shares)
    mixed = functools.reduce(
        jnp.add, [p[:HEAD_DIM].astype(F32) * s for p, s in zip(parts, shares)]
    )
    return mixed / total, top + jnp.log2(total)


def merge_body(*refs):
    ins, out = refs[:-1], refs[-1]
    width = out.shape[2]
    for i in range(out.shape[0]):
        mixed, lse = merge([r[:, i * width : i * width + width] for r in ins])
        out[i, :HEAD_DIM] = mixed.astype(BF)
        out[i, HEAD_DIM:] = write_rim(lse).astype(BF)


def join_body(mine, passing, out):
    mixed, lse = merge([mine[...], passing[...]])
    out[:HEAD_DIM] = mixed.astype(BF)
    out[HEAD_DIM:] = write_rim(lse).astype(BF)


def last_body(ins, out):
    heads = [merge([ins[a * B + b] for a in range(A)])[0] for b in range(B)]
    out[...] = jnp.concatenate(heads, axis=0).T.astype(BF)


def step(part, shift):
    return lax.ppermute(part, "y", [(i, (i + shift) % Y) for i in range(Y)])


def local(queries, keys, values):
    count = queries.shape[0]
    block = count // Y
    ranks = lax.axis_size("head") * B
    tokens = keys.shape[0]
    part = tokens // PACKS
    sent = pl.pallas_call(
        pack_body,
        grid=(PACKS,),
        in_specs=[pl.BlockSpec((part, keys.shape[1]), lambda i: (i, 0))] * 2,
        out_specs=pl.BlockSpec((ranks, part, 128), lambda i: (0, i, 0)),
        out_shape=jax.ShapeDtypeStruct((ranks, tokens, 128), BF),
        name="pack",
    )(keys, values)
    pairs = lax.all_to_all(sent, ("b", "head"), 0, 0, tiled=True).reshape(ranks * tokens, 128)
    columns, query_lengths = call(
        turn_body, (queries,), (jax.ShapeDtypeStruct((128, count), BF), LENGTHS), "turn"
    )
    turned, key_lengths = call(
        prep_body,
        (pairs,),
        (jax.ShapeDtypeStruct((ROWS, ranks * tokens), BF), LENGTHS),
        "prep",
    )
    lengths = (query_lengths, key_lengths)
    far = step(attend(2, columns, pairs, turned, lengths, block), 1)
    right = attend(1, columns, pairs, turned, lengths, block)
    columns, right = lax.optimization_barrier((columns, right))
    left = attend(3, columns, pairs, turned, lengths, block)
    right, left = lax.optimization_barrier((right, left))
    right = call(join_body, (right, far), jax.ShapeDtypeStruct((ROWS, block), BF), "join")
    columns, right, left = lax.optimization_barrier((columns, right, left))
    right, left = step(right, 1), step(left, 3)
    own = attend(0, columns, pairs, turned, lengths, block)
    width = block // (A * B)
    pieces = call(
        merge_body,
        (own, right, left),
        jax.ShapeDtypeStruct((A * B, ROWS, width), BF),
        "merge",
    )
    pieces = lax.all_to_all(pieces, ("a", "b"), 0, 0, tiled=True)
    return call(last_body, (pieces,), jax.ShapeDtypeStruct((width, 128), BF), "last")


def solution(mesh):
    fine = Mesh(mesh.devices.reshape(Y, A, B, -1), ("y", "a", "b", "head"))
    frame = ("y", "a", "b")
    placed = (P(None, "head"), P((*frame, "head"), None), P((*frame, "head"), None))
    return jax.shard_map(
        local, mesh=fine, in_specs=placed, out_specs=P(frame, "head"), check_vma=False
    )
```
